768 devices in a mesh: block: 32 (over y_lo, x, core), walker: 24 (over z, y_hi).
Axes of the slice: x: 4, y: 8 (y_hi: 2, y_lo: 4; y = y_hi * 4 + y_lo), z: 12, core: 2. Of those that a mesh axis runs over, the one named last changes fastest.
Arguments:
- green: bfloat16 [120, 294912], P('walker', 'block'), may hold values from -6 to 6
- chol: bfloat16 [256, 192, 1536], P('block'), may hold values from -0.15625 to 0.15625
- counts: int32 [24], replicated, may hold values from 1 to 5, as said below
- move_slot: int32 [24, 2], replicated, may hold values from -1 to 4, as said below
- move_dest: int32 [24, 2], replicated, may hold values from -1 to 23, as said below
Outputs:
- new_green: bfloat16 [72, 294912], P('walker', 'block')
- energy: float32 [72], P('walker')
The draws below stay inside these ranges and needn't reach their ends.
Inputs may be any that keep to these rules, and one draw needn't show every extreme that they name: On every device, counts minus the walkers it sends plus the walkers it receives equals 3; in every draw some device has count 5 and some device has count 1. `move_slot`: in each row the entries >= 0 come first, are distinct, and name live slots of that device; the rest are -1. `move_dest`: -1 exactly where move_slot is -1, else another device's index; from one device at most 1 walker goes to any one device, and some device sends that many to one.
All inputs are finite; a program needn't handle non-finite values.
Results may differ from the reference program's by a relative error of at most 0.0004.
Values may be sent and summed in bfloat16 or wider, within the bound.
A program may use at most 32 MiB of HBM per device.

```python
import jax
import jax.numpy as jnp
from jax import lax

NORB = 1536
NOCC = 192
MOVE = 2
BAL = 3
WSLOT = 5
GFLAT = 294912
NCHOL = 256
W_IN = 120
N_WALKER = 24


def population(key):
    base_key = jax.random.fold_in(key, 7)
    key_cycle, key_out, key_slot = jax.random.split(base_key, 3)
    walker_total = N_WALKER
    device_ids = jnp.arange(walker_total, dtype=jnp.int32)
    cycle_scores = jax.random.randint(key_cycle, (walker_total,), 0, 1 << 20).astype(jnp.int32) * walker_total + device_ids
    cycle_order = jnp.argsort(cycle_scores, stable=True).astype(jnp.int32)
    places = jnp.arange(walker_total, dtype=jnp.int32)
    out_by_place = jax.random.randint(key_out, (walker_total,), 0, MOVE + 1).astype(jnp.int32)
    out_by_place = jnp.where((places >= 1) & (places <= MOVE), MOVE, out_by_place)
    zero_place = (places == 0) | (places == MOVE + 1) | (places >= walker_total - MOVE + 1)
    out_by_place = jnp.where(zero_place, 0, out_by_place).astype(jnp.int32)
    place_of = jnp.zeros((walker_total,), jnp.int32).at[cycle_order].set(places)
    outgoing = out_by_place[place_of]
    move_ids = jnp.arange(MOVE, dtype=jnp.int32)
    dest_all = cycle_order[(place_of[:, None] + 1 + move_ids[None, :] % (walker_total - 1)) % walker_total]
    active = move_ids[None, :] < outgoing[:, None]
    arriving = jnp.sum(((dest_all[:, :, None] == device_ids[None, None, :]) & active[:, :, None]).astype(jnp.int32), axis=(0, 1))
    counts = (BAL + outgoing - arriving).astype(jnp.int32)
    slot_ids = jnp.arange(WSLOT, dtype=jnp.int32)
    scores = jax.random.randint(key_slot, (walker_total, WSLOT), 0, 4096).astype(jnp.int32) * WSLOT + slot_ids[None, :]
    scores = jnp.where(slot_ids[None, :] < counts[:, None], scores, scores + 8192 * WSLOT)
    forced = (place_of[:, None] == 1) & (slot_ids[None, :] == WSLOT - 1)
    scores = jnp.where(forced, -1, scores)
    picked = jnp.argsort(scores, axis=1, stable=True)[:, :MOVE].astype(jnp.int32)
    slot_list = jnp.where(active, picked, -1).astype(jnp.int32)
    dest_list = jnp.where(active, dest_all, -1).astype(jnp.int32)
    return (counts, slot_list, dest_list)


def draw_counts(key, part):
    return population(key)[0]


def draw_move_slot(key, part):
    return population(key)[1]


def draw_move_dest(key, part):
    return population(key)[2]


def level_of(stream_key, dims, cuts, smallest, top_value):
    gain = 1.0
    for dim, shards_of in cuts:
        draws = jax.random.uniform(jax.random.fold_in(jax.random.fold_in(stream_key, 6), dim), (shards_of,), jnp.float32, smallest / len(cuts), top_value / len(cuts))
        gain = gain * jnp.repeat(jnp.exp(draws), dims[dim] // shards_of).reshape((-1,) + (1,) * (len(dims) - 1 - dim))
    return gain


def noise(stream_key, extent, width, reach, cuts=(), held_as=jnp.bfloat16):
    level = level_of(stream_key, extent, cuts, -0.22, 0.18) if cuts else 1.0
    values = jax.random.normal(stream_key, extent, jnp.float32) * width * level
    return jnp.minimum(jnp.maximum(values, -reach), reach).astype(held_as)


def setup_inputs(seed: int = 0) -> dict:
    streams_of = jax.random.split(jax.random.key(seed), 6)
    green = noise(streams_of[0], (W_IN, GFLAT), 1.0, 6.0, ((0, 24), (1, 32)))
    chol = noise(streams_of[1], (NCHOL, NOCC, NORB), NORB ** -0.5, 0.15625, ((0, 32),))
    counts = draw_counts(jax.random.fold_in(streams_of[5], 71), 0)
    move_slot = draw_move_slot(jax.random.fold_in(streams_of[5], 71), 0)
    move_dest = draw_move_dest(jax.random.fold_in(streams_of[5], 71), 0)
    return {"green": green, "chol": chol, "counts": counts, "move_slot": move_slot, "move_dest": move_dest}


def layout(counts, move_slot, move_dest, target):
    slot_ids = jnp.arange(WSLOT, dtype=jnp.int32)
    device_ids = jnp.arange(N_WALKER, dtype=jnp.int32)
    move_ids = jnp.arange(MOVE, dtype=jnp.int32)
    occupied = slot_ids[None, :] < counts[:, None]
    leaving = jnp.any(move_slot[:, :, None] == slot_ids[None, None, :], axis=1)
    staying = (occupied & jnp.logical_not(leaving))[target]
    far_key = jnp.int32(1 << 20)
    stay_keys = jnp.where(staying, slot_ids, far_key)
    arrive_keys = jnp.where(move_dest == target, WSLOT + device_ids[:, None] * MOVE + move_ids[None, :], far_key).reshape(-1)
    stay_rows = target * WSLOT + slot_ids
    arrive_rows = (device_ids[:, None] * WSLOT + jnp.maximum(move_slot, 0)).reshape(-1)
    sort_keys = jnp.concatenate([stay_keys, arrive_keys.astype(jnp.int32)])
    source_rows = jnp.concatenate([stay_rows, arrive_rows.astype(jnp.int32)])
    ranking = jnp.argsort(sort_keys, stable=True)[:BAL]
    return source_rows[ranking].astype(jnp.int32)


def reference(green, chol, counts, move_slot, move_dest):
    row_index = jnp.concatenate([layout(counts, move_slot, move_dest, target) for target in range(N_WALKER)])
    new_green = green[row_index]
    chol_float = chol.astype(jnp.float32)
    energy_scale = 0.5 / (NOCC * (NCHOL ** 0.5))

    def walker_energy(walker_row):
        green_mat = walker_row.astype(jnp.float32).reshape(NOCC, NORB)
        transfer = jnp.einsum("gip,jp->gij", chol_float, green_mat, precision=lax.Precision.HIGHEST)
        return jnp.sum(transfer * jnp.swapaxes(transfer, 1, 2))

    energy = -energy_scale * lax.map(walker_energy, new_green)
    return new_green, energy
```

```python
import math

import jax
import jax.numpy as jnp
from jax import lax
from jax.experimental import pallas as pl
from jax.experimental.pallas import tpu as pltpu
from jax.sharding import PartitionSpec as P

MESH = pl.DeviceIdType.MESH
NT = (((1,), (1,)), ((), ()))
BF = jnp.bfloat16
F32 = jnp.float32
SLOTS = 5
KEEP = 3
X, Y, YH, Z = 4, 4, 2, 12
ROWS = 6
NORB = 1536
NOCC = 192
SHARE = ROWS * NORB
LINES = SHARE // 128


def trace_half(t):
    acc = jnp.zeros((64, 128), F32)
    corners = []
    for pair in range(2):
        t0 = t[:, 384 * pair : 384 * pair + 128]
        t1 = t[:, 384 * pair + 128 : 384 * pair + 256]
        t2 = t[:, 384 * pair + 256 : 384 * pair + 384]
        for a in (t0[0:128], t2[0:128]):
            m = a * a.T
            acc = acc + m[0:64] + m[64:128]
        b = t1[0:128].T
        acc = acc + 2.0 * (b[0:64] * t0[128:192] + b[64:128] * t2[128:192])
        corners.append(t1[128:192])
    e = jnp.concatenate(corners, 0)
    et = e.T
    low = lax.broadcasted_iota(jnp.int32, (64, 128), 1) < 64
    r0 = pltpu.roll(et[0:64], 64, 1)
    r1 = pltpu.roll(et[64:128], 64, 1)
    acc = acc + e[0:64] * jnp.where(low, et[0:64], r1)
    return acc + e[64:128] * jnp.where(low, r0, et[64:128])


def kernel(
    green, chol, counts, mslot, mdest, new_ref, en_ref,
    gin, x32, s32, g72, line, n32, gbuf, lbuf, xsend, xrecv, cbuf, gc, tbuf, ea, eb, ec,
    local_sem, send_sem, rg, rl, ra, rb, rc, rx,
):
    blk = lax.axis_index("block")
    wlk = lax.axis_index("walker")
    c = lax.rem(blk, 2)
    x = lax.rem(lax.div(blk, 2), X)
    y = lax.div(blk, 2 * X)
    yh = lax.rem(wlk, YH)
    z = lax.div(wlk, YH)
    oc = 1 - c
    xp, xm, xo = lax.rem(x + 1, X), lax.rem(x + X - 1, X), lax.rem(x + 2, X)
    ys = [y, y + 1 - 2 * lax.rem(y, 2), y + 2 - 4 * lax.div(y, 2), 3 - y]

    def shard(yy, xx, cc):
        return (yy * X + xx) * 2 + cc

    def dev(yy, xx, cc, zz, hh):
        return {"block": shard(yy, xx, cc), "walker": zz * YH + hh}

    def zat(offset):
        return lax.rem(z + offset + Z, Z)

    green_copy = pltpu.make_async_copy(green, gin, local_sem.at[0])
    green_copy.start()
    chol_copy = pltpu.make_async_copy(chol, cbuf, local_sem.at[1])
    chol_copy.start()

    xc_peers = [dev(y, lax.rem(x + dx, X), cc, z, yh) for dx in range(X) for cc in (c, oc)][1:]
    y_peers = [dev(ys[i], x, c, z, yh) for i in range(1, Y)]
    y_peers += [dev(ys[i], x, c, z, 1 - yh) for i in range(Y)]
    z_peers = [dev(y, x, c, zat(i), yh) for i in range(1, Z)]
    peers = xc_peers + y_peers + z_peers
    barrier = pltpu.get_barrier_semaphore()
    for peer in peers:
        pl.semaphore_signal(barrier, inc=1, device_id=peer, device_id_type=MESH)

    sent = []

    def send(src, dst, rsem, device):
        copy = pltpu.make_async_remote_copy(
            src_ref=src, dst_ref=dst, send_sem=send_sem.at[len(sent)], recv_sem=rsem,
            device_id=device, device_id_type=MESH,
        )
        copy.start()
        sent.append(copy)

    def arrive(dst, rsem, device):
        pltpu.make_async_remote_copy(
            src_ref=dst, dst_ref=dst, send_sem=send_sem.at[0], recv_sem=rsem,
            device_id=device, device_id_type=MESH,
        ).wait_recv()

    green_copy.wait()
    x32[0:SLOTS, :] = gin[...].astype(F32)
    s32[24:32, :] = jnp.zeros((8, NORB), F32)
    for r in range(ROWS):
        s32[SLOTS * r : SLOTS * r + SLOTS, :] = x32[0:SLOTS, NORB * r : NORB * r + NORB]
    gbuf[blk] = s32[...].astype(BF)

    for s in range(SLOTS):
        for r in range(LINES):
            g72[s, r : r + 1, :] = x32[s : s + 1, 128 * r : 128 * r + 128]
    for j in range(2):
        lbuf[z, j] = g72[jnp.maximum(mslot[wlk, j], 0)].astype(BF)

    partner = wlk + 1 - 2 * yh
    zero = jnp.int32(0)

    def scan(d, carry):
        own, n, other, m = carry
        for j in range(2):
            dest = mdest[d, j]
            live = mslot[d, j] >= 0
            hit = jnp.where(live & (dest == wlk), 1, 0)
            own = tuple(jnp.where((hit == 1) & (n == a), d * 2 + j, own[a]) for a in range(KEEP))
            n = n + hit
            hit = jnp.where(live & (dest == partner), 1, 0)
            other = tuple(jnp.where((hit == 1) & (m == a), d * 2 + j, other[a]) for a in range(KEEP))
            m = m + hit
        return own, n, other, m

    own, _, other, _ = lax.fori_loop(
        0, Z * YH, scan, ((zero,) * KEEP, zero, (zero,) * KEEP, zero)
    )
    stay_total = zero
    stay = [zero] * KEEP
    for s in range(SLOTS):
        hit = jnp.where((s < counts[wlk]) & (mslot[wlk, 0] != s) & (mslot[wlk, 1] != s), 1, 0)
        stay = [jnp.where((hit == 1) & (stay_total == t), s, stay[t]) for t in range(KEEP)]
        stay_total = stay_total + hit

    pl.semaphore_wait(barrier, len(peers))

    xpd, xmd, pd = dev(y, xp, c, z, yh), dev(y, xm, c, z, yh), dev(y, x, oc, z, yh)
    zpd, zmd = dev(y, x, c, zat(1), yh), dev(y, x, c, zat(-1), yh)

    def forward(i, first):
        b = shard(ys[i], x, c)
        if not first:
            arrive(gbuf.at[b], rg.at[b, 0], pd)
        send(gbuf.at[b], gbuf.at[b], rg.at[b, 0], xpd)
        send(gbuf.at[b], gbuf.at[b], rg.at[b, 0], xmd)
        if first:
            for k in range(1, Y):
                send(gbuf.at[b], gbuf.at[b], rg.at[b, 0], y_peers[k - 1])
        send(gbuf.at[b], gbuf.at[b], rg.at[b, 0], pd)

    def relay(i):
        b = shard(ys[i], xm, c)
        arrive(gbuf.at[b], rg.at[b, 0], pd)
        send(gbuf.at[b, 0:16], gbuf.at[b, 0:16], rg.at[b, 0], xpd)
        send(gbuf.at[b], gbuf.at[b], rg.at[b, 0], pd)
        b = shard(ys[i], xp, c)
        arrive(gbuf.at[b], rg.at[b, 0], pd)
        send(gbuf.at[b, 16:32], gbuf.at[b, 16:32], rg.at[b, 1], xmd)
        send(gbuf.at[b], gbuf.at[b], rg.at[b, 0], pd)

    def opposite(i):
        b = shard(ys[i], xo, c)
        arrive(gbuf.at[b, 0:16], rg.at[b, 0], pd)
        arrive(gbuf.at[b, 16:32], rg.at[b, 1], pd)
        send(gbuf.at[b], gbuf.at[b], rg.at[b, 0], pd)

    def other_core(i):
        for xx in (x, xm, xp, xo):
            b = shard(ys[i], xx, oc)
            arrive(gbuf.at[b], rg.at[b, 0], pd)

    def zsend(t):
        lo, hi = zat(-(t - 1)), zat(t - 1)
        if t < 6:
            send(lbuf.at[lo], lbuf.at[lo], rl.at[lo, 0], zpd)
            send(lbuf.at[hi], lbuf.at[hi], rl.at[hi, 0], zmd)
        else:
            send(lbuf.at[lo, 0], lbuf.at[lo, 0], rl.at[lo, 0], zpd)
            send(lbuf.at[hi, 1], lbuf.at[hi, 1], rl.at[hi, 1], zmd)

    def zstep(t):
        lo, hi = zat(-t), zat(t)
        if t < 6:
            arrive(lbuf.at[lo], rl.at[lo, 0], pd)
            arrive(lbuf.at[hi], rl.at[hi, 0], pd)
            zsend(t + 1)
        else:
            arrive(lbuf.at[lo, 0], rl.at[lo, 0], pd)
            arrive(lbuf.at[lo, 1], rl.at[lo, 1], pd)

    row_id = lax.broadcasted_iota(jnp.int32, (240, 256), 0)
    col_id = lax.broadcasted_iota(jnp.int32, (240, 256), 1)
    inner = jnp.bitwise_and(col_id, 31)
    rr = jnp.right_shift(inner * 13, 6)
    target = (inner - SLOTS * rr) * 48 + jnp.right_shift(col_id, 5) * ROWS + rr
    pick = jnp.where((row_id == target) & (inner < 30), 1.0, 0.0).astype(BF)

    def compute(i):
        base = ys[i] * 8
        a = gbuf[pl.ds(base, 8)].reshape(256, NORB)
        for kc in range(6):
            cols = slice(256 * kc, 256 * kc + 256)
            gc[:, cols] = jnp.dot(pick, a[:, cols], preferred_element_type=F32).astype(BF)
        rows = pl.ds(pl.multiple_of(ys[i] * 48, 16), 48)

        def half(h, _):
            g = 4 * h
            w = jnp.concatenate(
                [
                    cbuf[g], cbuf[g + 1, 128:192], cbuf[g + 1, 0:128],
                    cbuf[g + 2], cbuf[g + 3, 128:192], cbuf[g + 3, 0:128],
                ],
                0,
            )
            t = lax.dot_general(gc[...], w, NT, preferred_element_type=F32)
            for s in range(SLOTS):
                tbuf[h, s, rows, :] = t[48 * s : 48 * s + 48]
            return 0

        lax.fori_loop(0, 2, half, 0)

    forward(0, True)
    zsend(1)
    forward(1, False)
    relay(0)
    zstep(1)
    opposite(0)
    zstep(2)
    forward(2, False)
    relay(1)
    zstep(3)
    other_core(0)
    chol_copy.wait()
    compute(0)
    opposite(1)
    zstep(4)
    forward(3, False)
    relay(2)
    other_core(1)
    compute(1)
    zstep(5)
    opposite(2)
    relay(3)
    other_core(2)
    compute(2)
    zstep(6)
    for a in range(KEEP):
        xsend[a] = lbuf[lax.div(other[a], 4), lax.rem(other[a], 2)]
    opposite(3)
    send(xsend, xrecv, rx.at[0], dev(y, x, c, z, 1 - yh))
    other_core(3)
    compute(3)

    lane = lax.broadcasted_iota(jnp.int32, (1, 128), 1)

    def slot_trace(s, part):
        tot = trace_half(tbuf[0, s]) + trace_half(tbuf[1, s])
        value = jnp.sum(jnp.sum(tot, axis=0, keepdims=True), axis=1, keepdims=True)
        return jnp.where(lane == s, value, part)

    part = lax.fori_loop(0, SLOTS, slot_trace, jnp.zeros((1, 128), F32))

    def exchange(buf, sem, me, value, targets, sources):
        buf[me] = value
        for device in targets:
            send(buf.at[me], buf.at[me], sem.at[me], device)
        for src in sources:
            arrive(buf.at[src], sem.at[src], pd)

    exchange(
        ea, ra, x * 2 + c, part, xc_peers,
        [lax.rem(x + dx, X) * 2 + cc for dx in range(X) for cc in (c, oc)][1:],
    )
    total = ea[0]
    for i in range(1, 2 * X):
        total = total + ea[i]
    exchange(
        eb, rb, yh * Y + y, total, y_peers,
        [yh * Y + ys[i] for i in range(1, Y)] + [(1 - yh) * Y + ys[i] for i in range(Y)],
    )
    first = eb[0] + eb[1] + eb[2] + eb[3]
    second = eb[4] + eb[5] + eb[6] + eb[7]
    exchange(
        ec, rc, z, first + pltpu.roll(second, 8, 1), z_peers, [zat(i) for i in range(1, Z)]
    )

    arrive(xrecv, rx.at[0], pd)
    scale = 0.5 / (NOCC * math.sqrt(256.0))
    for t in range(KEEP):
        stays = t < stay_total
        rank = jnp.clip(t - stay_total, 0, KEEP - 1)
        pick_id = own[0]
        for a in range(1, KEEP):
            pick_id = jnp.where(rank == a, own[a], pick_id)
        src_z = lax.div(pick_id, 4)
        src_h = lax.rem(lax.div(pick_id, 2), 2)
        src_j = lax.rem(pick_id, 2)
        moved = jnp.where(src_h == yh, lbuf[src_z, src_j].astype(F32), xrecv[rank].astype(F32))
        line[t] = jnp.where(stays, g72[stay[t]], moved)
        for r in range(LINES):
            n32[t : t + 1, 128 * r : 128 * r + 128] = line[t, r : r + 1, :]
        from_z = jnp.where(stays, z, src_z)
        from_h = jnp.where(stays, yh, src_h)
        from_s = jnp.where(stays, stay[t], jnp.maximum(mslot[src_z * 2 + src_h, src_j], 0))
        row = ec[from_z]
        en_ref[t] = -scale * jnp.sum(jnp.where(lane == from_h * 8 + from_s, row, 0.0))
    new_ref[...] = n32[0:KEEP, :].astype(BF)

    for copy in sent:
        copy.wait_send()


def body(green, chol, counts, move_slot, move_dest):
    hbm = pl.BlockSpec(memory_space=pl.ANY)
    smem = pl.BlockSpec(memory_space=pltpu.SMEM)
    return pl.pallas_call(
        kernel,
        out_shape=(
            jax.ShapeDtypeStruct((KEEP, SHARE), BF),
            jax.ShapeDtypeStruct((KEEP,), F32),
        ),
        in_specs=[hbm, hbm, smem, smem, smem],
        out_specs=(pl.BlockSpec(memory_space=pltpu.VMEM), smem),
        scratch_shapes=[
            pltpu.VMEM((SLOTS, SHARE), BF),
            pltpu.VMEM((8, SHARE), F32),
            pltpu.VMEM((32, NORB), F32),
            pltpu.VMEM((SLOTS, LINES, 128), F32),
            pltpu.VMEM((KEEP, LINES, 128), F32),
            pltpu.VMEM((8, SHARE), F32),
            pltpu.VMEM((32, 32, NORB), BF),
            pltpu.VMEM((Z, 2, LINES, 128), BF),
            pltpu.VMEM((KEEP, LINES, 128), BF),
            pltpu.VMEM((KEEP, LINES, 128), BF),
            pltpu.VMEM((8, NOCC, NORB), BF),
            pltpu.VMEM((240, NORB), BF),
            pltpu.VMEM((2, SLOTS, NOCC, 768), F32),
            pltpu.VMEM((2 * X, 1, 128), F32),
            pltpu.VMEM((YH * Y, 1, 128), F32),
            pltpu.VMEM((Z, 1, 128), F32),
            pltpu.SemaphoreType.DMA((2,)),
            pltpu.SemaphoreType.DMA((80,)),
            pltpu.SemaphoreType.DMA((32, 2)),
            pltpu.SemaphoreType.DMA((Z, 2)),
            pltpu.SemaphoreType.DMA((2 * X,)),
            pltpu.SemaphoreType.DMA((YH * Y,)),
            pltpu.SemaphoreType.DMA((Z,)),
            pltpu.SemaphoreType.DMA((1,)),
        ],
        compiler_params=pltpu.CompilerParams(
            collective_id=0, has_side_effects=True, vmem_limit_bytes=60 << 20
        ),
        name="exchange_energy",
    )(green, chol, counts, move_slot, move_dest)


def solution(mesh):
    in_specs = (P("walker", "block"), P("block", None, None), P(), P(), P())
    out_specs = (P("walker", "block"), P("walker"))
    return jax.shard_map(body, mesh=mesh, in_specs=in_specs, out_specs=out_specs, check_vma=False)
```

```python
import math

import jax
import jax.numpy as jnp
from jax import lax
from jax.experimental import pallas as pl
from jax.experimental.pallas import tpu as pltpu
from jax.sharding import PartitionSpec as P

MESH = pl.DeviceIdType.MESH
NT = (((1,), (1,)), ((), ()))
BF = jnp.bfloat16
F32 = jnp.float32
SLOTS = 5
KEEP = 3
X, Y, YH, Z = 4, 4, 2, 12
ROWS = 6
NORB = 1536
NOCC = 192
SHARE = ROWS * NORB
LINES = SHARE // 128


def trace_half(t):
    acc = jnp.zeros((64, 128), F32)
    corners = []
    for pair in range(2):
        t0 = t[:, 384 * pair : 384 * pair + 128]
        t1 = t[:, 384 * pair + 128 : 384 * pair + 256]
        t2 = t[:, 384 * pair + 256 : 384 * pair + 384]
        for a in (t0[0:128], t2[0:128]):
            m = a * a.T
            acc = acc + m[0:64] + m[64:128]
        b = t1[0:128].T
        acc = acc + 2.0 * (b[0:64] * t0[128:192] + b[64:128] * t2[128:192])
        corners.append(t1[128:192])
    e = jnp.concatenate(corners, 0)
    et = e.T
    low = lax.broadcasted_iota(jnp.int32, (64, 128), 1) < 64
    r0 = pltpu.roll(et[0:64], 64, 1)
    r1 = pltpu.roll(et[64:128], 64, 1)
    acc = acc + e[0:64] * jnp.where(low, et[0:64], r1)
    return acc + e[64:128] * jnp.where(low, r0, et[64:128])


def kernel(
    green, chol, counts, mslot, mdest, new_ref, en_ref,
    gin, x32, s32, g72, line, n32, nout, gbuf, lbuf, xsend, xrecv, cbuf, gc, tbuf, ea, eb, ec,
    local_sem, send_sem, rg, rl, ra, rb, rc, rx, hyz,
):
    blk = lax.axis_index("block")
    wlk = lax.axis_index("walker")
    c = lax.rem(blk, 2)
    x = lax.rem(lax.div(blk, 2), X)
    y = lax.div(blk, 2 * X)
    yh = lax.rem(wlk, YH)
    z = lax.div(wlk, YH)
    oc = 1 - c
    xp, xm, xo = lax.rem(x + 1, X), lax.rem(x + X - 1, X), lax.rem(x + 2, X)
    y1 = y - 1 + 2 * lax.div(Y - y, Y)
    y3 = (Y - 1) * (1 - lax.div(y, 2))
    ys = [y, y1, 6 - y - y1 - y3, y3]

    def shard(yy, xx, cc):
        return (yy * X + xx) * 2 + cc

    def dev(yy, xx, cc, zz, hh):
        return {"block": shard(yy, xx, cc), "walker": zz * YH + hh}

    def zat(offset):
        return lax.rem(z + offset + Z, Z)

    green_copy = pltpu.make_async_copy(green, gin, local_sem.at[0])
    green_copy.start()
    chol_copy = pltpu.make_async_copy(chol, cbuf, local_sem.at[1])
    chol_copy.start()

    y8 = yh * Y + y

    def ydev(offset):
        at = lax.rem(y8 + offset + YH * Y, YH * Y)
        return dev(lax.rem(at, Y), x, c, z, lax.div(at, Y))

    xc_peers = [dev(y, lax.rem(x + dx, X), cc, z, yh) for dx in range(X) for cc in (c, oc)][1:]
    y_peers = [ydev(i) for i in range(1, YH * Y)]
    z_peers = [dev(y, x, c, zat(i), yh) for i in range(1, Z)]
    xpd, xmd, pd = dev(y, xp, c, z, yh), dev(y, xm, c, z, yh), dev(y, x, oc, z, yh)
    ypd, ymd = ydev(1), ydev(-1)
    zpd, zmd = dev(y, x, c, zat(1), yh), dev(y, x, c, zat(-1), yh)
    near = [xpd, xmd, pd, ypd, ymd, zpd, zmd]
    barrier = pltpu.get_barrier_semaphore()
    for peer in near:
        pl.semaphore_signal(barrier, inc=1, device_id=peer, device_id_type=MESH)

    sent = []

    def send(src, dst, rsem, device, cond=None):
        index = len(sent)

        def make():
            return pltpu.make_async_remote_copy(
                src_ref=src(), dst_ref=dst(), send_sem=send_sem.at[index], recv_sem=rsem(),
                device_id=device, device_id_type=MESH,
            )

        sent.append((make, cond))
        if cond is None:
            make().start()
        else:
            pl.when(cond)(lambda: make().start())

    def both(ref, rsem, device, cond=None):
        send(ref, ref, rsem, device, cond)

    def arrive(dst, rsem, device):
        pltpu.make_async_remote_copy(
            src_ref=dst, dst_ref=dst, send_sem=send_sem.at[0], recv_sem=rsem,
            device_id=device, device_id_type=MESH,
        ).wait_recv()

    green_copy.wait()
    x32[0:SLOTS, :] = gin[...].astype(F32)
    s32[24:32, :] = jnp.zeros((8, NORB), F32)
    for r in range(ROWS):
        s32[SLOTS * r : SLOTS * r + SLOTS, :] = x32[0:SLOTS, NORB * r : NORB * r + NORB]
    gbuf[blk] = s32[...].astype(BF)

    pl.semaphore_wait(barrier, len(near))

    def half(b, h):
        return lambda: gbuf.at[b, 16 * h : 16 * h + 16]

    def whole(b):
        return lambda: gbuf.at[b]

    def sem(b, h):
        return lambda: rg.at[b, h]

    def forward(i):
        b = shard(ys[i], x, c)
        if i == 0:
            up, down = y < Y - 1, y > 0
        else:
            up, down = (ys[i] < y) & (y < Y - 1), (ys[i] > y) & (y > 0)
        for h in range(2):
            if i > 0:
                arrive(gbuf.at[b, 16 * h : 16 * h + 16], rg.at[b, h], pd)
            both(half(b, h), sem(b, h), ypd, up)
            both(half(b, h), sem(b, h), ymd, down)
            both(half(b, h), sem(b, h), xpd)
        for h in (1, 0):
            both(half(b, h), sem(b, h), xmd)
        both(whole(b), sem(b, 0), pd)

    def relay(i):
        b = shard(ys[i], xm, c)
        arrive(gbuf.at[b, 0:16], rg.at[b, 0], pd)
        both(half(b, 0), sem(b, 0), xpd)
        b = shard(ys[i], xp, c)
        arrive(gbuf.at[b, 16:32], rg.at[b, 1], pd)
        both(half(b, 1), sem(b, 1), xmd)

    def rest(i):
        b = shard(ys[i], xm, c)
        arrive(gbuf.at[b, 16:32], rg.at[b, 1], pd)
        both(whole(b), sem(b, 0), pd)
        b = shard(ys[i], xp, c)
        arrive(gbuf.at[b, 0:16], rg.at[b, 0], pd)
        both(whole(b), sem(b, 0), pd)
        b = shard(ys[i], xo, c)
        arrive(gbuf.at[b, 0:16], rg.at[b, 0], pd)
        arrive(gbuf.at[b, 16:32], rg.at[b, 1], pd)
        both(whole(b), sem(b, 0), pd)

    def other_core(i):
        for xx in (x, xm, xp, xo):
            b = shard(ys[i], xx, oc)
            arrive(gbuf.at[b], rg.at[b, 0], pd)

    def zsend():
        for device in z_peers:
            both(lambda: lbuf.at[z], lambda: rl.at[z], device)

    def zarrive():
        for i in range(1, Z):
            arrive(lbuf.at[zat(i)], rl.at[zat(i)], pd)

    def hello(i):
        for device in (ypd, ymd, zpd, zmd):
            pl.semaphore_signal(hyz.at[i], inc=1, device_id=device, device_id_type=MESH)

    def heard(i):
        pl.semaphore_wait(hyz.at[i], 4)

    forward(0)
    hello(0)

    for s in range(SLOTS):
        for r in range(LINES):
            g72[s, r : r + 1, :] = x32[s : s + 1, 128 * r : 128 * r + 128]
    for j in range(2):
        lbuf[z, j] = g72[jnp.maximum(mslot[j, wlk], 0)].astype(BF)

    partner = wlk + 1 - 2 * yh
    zero = jnp.int32(0)

    def scan(d, carry):
        own, n, other, m = carry
        for j in range(2):
            dest = mdest[j, d]
            live = mslot[j, d] >= 0
            hit = jnp.where(live & (dest == wlk), 1, 0)
            own = tuple(jnp.where((hit == 1) & (n == a), d * 2 + j, own[a]) for a in range(KEEP))
            n = n + hit
            hit = jnp.where(live & (dest == partner), 1, 0)
            other = tuple(jnp.where((hit == 1) & (m == a), d * 2 + j, other[a]) for a in range(KEEP))
            m = m + hit
        return own, n, other, m

    own, _, other, _ = lax.fori_loop(
        0, Z * YH, scan, ((zero,) * KEEP, zero, (zero,) * KEEP, zero)
    )
    stay_total = zero
    stay = [zero] * KEEP
    for s in range(SLOTS):
        hit = jnp.where((s < counts[wlk]) & (mslot[0, wlk] != s) & (mslot[1, wlk] != s), 1, 0)
        stay = [jnp.where((hit == 1) & (stay_total == t), s, stay[t]) for t in range(KEEP)]
        stay_total = stay_total + hit

    row_id = lax.broadcasted_iota(jnp.int32, (240, 256), 0)
    col_id = lax.broadcasted_iota(jnp.int32, (240, 256), 1)
    inner = jnp.bitwise_and(col_id, 31)
    rr = jnp.right_shift(inner * 13, 6)
    target = (inner - SLOTS * rr) * 48 + jnp.right_shift(col_id, 5) * ROWS + rr
    pick = jnp.where((row_id == target) & (inner < 30), 1.0, 0.0).astype(BF)

    def gather_rows(i):
        a = gbuf[pl.ds(ys[i] * 8, 8)].reshape(256, NORB)
        for kc in range(6):
            cols = slice(256 * kc, 256 * kc + 256)
            gc[:, cols] = jnp.dot(pick, a[:, cols], preferred_element_type=F32).astype(BF)

    def multiply(i, h):
        rows = pl.ds(pl.multiple_of(ys[i] * 48, 16), 48)
        g = 4 * h
        w = jnp.concatenate(
            [
                cbuf[g], cbuf[g + 1, 128:192], cbuf[g + 1, 0:128],
                cbuf[g + 2], cbuf[g + 3, 128:192], cbuf[g + 3, 0:128],
            ],
            0,
        )
        t = lax.dot_general(gc[...], w, NT, preferred_element_type=F32)
        for s in range(SLOTS):
            tbuf[h, s, rows, :] = t[48 * s : 48 * s + 48]

    heard(0)
    hello(1)
    forward(1)
    heard(1)
    hello(2)
    relay(0)
    heard(2)
    hello(3)
    rest(0)
    heard(3)
    hello(4)
    forward(2)
    heard(4)
    zsend()
    relay(1)
    other_core(0)
    chol_copy.wait()
    gather_rows(0)
    rest(1)
    multiply(0, 0)
    forward(3)
    multiply(0, 1)
    relay(2)
    other_core(1)
    gather_rows(1)
    rest(2)
    multiply(1, 0)
    relay(3)
    multiply(1, 1)
    other_core(2)
    gather_rows(2)
    rest(3)
    multiply(2, 0)
    multiply(2, 1)
    zarrive()
    for a in range(KEEP):
        xsend[a] = lbuf[lax.div(other[a], 4), lax.rem(other[a], 2)]
    other_core(3)
    gather_rows(3)
    send(lambda: xsend, lambda: xrecv, lambda: rx.at[0], dev(y, x, c, z, 1 - yh))
    multiply(3, 0)
    multiply(3, 1)

    lane = lax.broadcasted_iota(jnp.int32, (1, 128), 1)
    part = jnp.zeros((1, 128), F32)
    tots = [trace_half(tbuf[0, s]) for s in range(SLOTS)]
    for s in range(SLOTS):
        tot = tots[s] + trace_half(tbuf[1, s])
        value = jnp.sum(jnp.sum(tot, axis=0, keepdims=True), axis=1, keepdims=True)
        part = jnp.where(lane == s, value, part)

    def exchange(buf, sem, me, value, targets, sources):
        buf[me] = value
        for device in targets:
            both(lambda: buf.at[me], lambda: sem.at[me], device)
        for src in sources:
            arrive(buf.at[src], sem.at[src], pd)

    exchange(
        ea, ra, x * 2 + c, part, xc_peers,
        [lax.rem(x + dx, X) * 2 + cc for dx in range(X) for cc in (c, oc)][1:],
    )
    total = ea[0]
    for i in range(1, 2 * X):
        total = total + ea[i]
    exchange(
        eb, rb, y8, total, y_peers,
        [lax.rem(y8 + i, YH * Y) for i in range(1, YH * Y)],
    )
    first = eb[0] + eb[1] + eb[2] + eb[3]
    second = eb[4] + eb[5] + eb[6] + eb[7]
    row = first + pltpu.roll(second, 8, 1)
    ec[z] = row
    for device in z_peers:
        both(lambda: ec.at[z], lambda: rc.at[z], device)

    arrive(xrecv, rx.at[0], pd)
    scale = 0.5 / (NOCC * math.sqrt(256.0))
    found = []
    for t in range(KEEP):
        stays = t < stay_total
        rank = jnp.clip(t - stay_total, 0, KEEP - 1)
        pick_id = own[0]
        for a in range(1, KEEP):
            pick_id = jnp.where(rank == a, own[a], pick_id)
        src_z = lax.div(pick_id, 4)
        src_h = lax.rem(lax.div(pick_id, 2), 2)
        src_j = lax.rem(pick_id, 2)
        moved = jnp.where(src_h == yh, lbuf[src_z, src_j].astype(F32), xrecv[rank].astype(F32))
        line[t] = jnp.where(stays, g72[stay[t]], moved)
        for r in range(LINES):
            n32[t : t + 1, 128 * r : 128 * r + 128] = line[t, r : r + 1, :]
        from_z = jnp.where(stays, z, src_z)
        from_h = jnp.where(stays, yh, src_h)
        from_s = jnp.where(stays, stay[t], jnp.maximum(mslot[src_j, src_z * 2 + src_h], 0))
        found.append((from_z, from_h * 8 + from_s))
    nout[...] = n32[0:KEEP, :].astype(BF)
    new_copy = pltpu.make_async_copy(nout, new_ref, local_sem.at[2])
    new_copy.start()
    for i in range(1, Z):
        arrive(ec.at[zat(i)], rc.at[zat(i)], pd)
    for t, (from_z, at) in enumerate(found):
        en_ref[t] = -scale * jnp.sum(jnp.where(lane == at, ec[from_z], 0.0))
    new_copy.wait()

    for make, cond in sent:
        if cond is None:
            make().wait_send()
        else:
            pl.when(cond)(lambda make=make: make().wait_send())


def body(green, chol, counts, move_slot, move_dest):
    hbm = pl.BlockSpec(memory_space=pl.ANY)
    smem = pl.BlockSpec(memory_space=pltpu.SMEM)
    return pl.pallas_call(
        kernel,
        out_shape=(
            jax.ShapeDtypeStruct((KEEP, SHARE), BF),
            jax.ShapeDtypeStruct((KEEP,), F32),
        ),
        in_specs=[hbm, hbm, smem, smem, smem],
        out_specs=(hbm, smem),
        scratch_shapes=[
            pltpu.VMEM((SLOTS, SHARE), BF),
            pltpu.VMEM((8, SHARE), F32),
            pltpu.VMEM((32, NORB), F32),
            pltpu.VMEM((SLOTS, LINES, 128), F32),
            pltpu.VMEM((KEEP, LINES, 128), F32),
            pltpu.VMEM((8, SHARE), F32),
            pltpu.VMEM((KEEP, SHARE), BF),
            pltpu.VMEM((32, 32, NORB), BF),
            pltpu.VMEM((Z, 2, LINES, 128), BF),
            pltpu.VMEM((KEEP, LINES, 128), BF),
            pltpu.VMEM((KEEP, LINES, 128), BF),
            pltpu.VMEM((8, NOCC, NORB), BF),
            pltpu.VMEM((240, NORB), BF),
            pltpu.VMEM((2, SLOTS, NOCC, 768), F32),
            pltpu.VMEM((2 * X, 1, 128), F32),
            pltpu.VMEM((YH * Y, 1, 128), F32),
            pltpu.VMEM((Z, 1, 128), F32),
            pltpu.SemaphoreType.DMA((3,)),
            pltpu.SemaphoreType.DMA((120,)),
            pltpu.SemaphoreType.DMA((32, 2)),
            pltpu.SemaphoreType.DMA((Z,)),
            pltpu.SemaphoreType.DMA((2 * X,)),
            pltpu.SemaphoreType.DMA((YH * Y,)),
            pltpu.SemaphoreType.DMA((Z,)),
            pltpu.SemaphoreType.DMA((1,)),
            pltpu.SemaphoreType.REGULAR((5,)),
        ],
        compiler_params=pltpu.CompilerParams(
            collective_id=0, has_side_effects=True, vmem_limit_bytes=60 << 20
        ),
        name="exchange_energy",
    )(green, chol, counts, move_slot.T, move_dest.T)


def solution(mesh):
    in_specs = (P("walker", "block"), P("block", None, None), P(), P(), P())
    out_specs = (P("walker", "block"), P("walker"))
    return jax.shard_map(body, mesh=mesh, in_specs=in_specs, out_specs=out_specs, check_vma=False)
```

```python
import math

import jax
import jax.numpy as jnp
from jax import lax
from jax.experimental import pallas as pl
from jax.experimental.pallas import tpu as pltpu
from jax.sharding import PartitionSpec as P

MESH = pl.DeviceIdType.MESH
NT = (((1,), (1,)), ((), ()))
BF = jnp.bfloat16
F32 = jnp.float32
SLOTS = 5
KEEP = 3
X, Y, YH, Z = 4, 4, 2, 12
ROWS = 6
NORB = 1536
NOCC = 192
SHARE = ROWS * NORB
LINES = SHARE // 128


def trace_half(t):
    acc = jnp.zeros((64, 128), F32)
    corners = []
    for pair in range(2):
        t0 = t[:, 384 * pair : 384 * pair + 128]
        t1 = t[:, 384 * pair + 128 : 384 * pair + 256]
        t2 = t[:, 384 * pair + 256 : 384 * pair + 384]
        for a in (t0[0:128], t2[0:128]):
            m = a * a.T
            acc = acc + m[0:64] + m[64:128]
        b = t1[0:128].T
        acc = acc + 2.0 * (b[0:64] * t0[128:192] + b[64:128] * t2[128:192])
        corners.append(t1[128:192])
    e = jnp.concatenate(corners, 0)
    et = e.T
    low = lax.broadcasted_iota(jnp.int32, (64, 128), 1) < 64
    r0 = pltpu.roll(et[0:64], 64, 1)
    r1 = pltpu.roll(et[64:128], 64, 1)
    acc = acc + e[0:64] * jnp.where(low, et[0:64], r1)
    return acc + e[64:128] * jnp.where(low, r0, et[64:128])


def kernel(
    green, chol, counts, mslot, mdest, new_ref, en_ref,
    gin, x32, s32, g72, line, n32, nout, gbuf, lbuf, xsend, xrecv, cbuf, gc, tbuf, ea, eb, ec,
    local_sem, send_sem, rg, rl, ra, rb, rc, rx, hyz,
):
    blk = lax.axis_index("block")
    wlk = lax.axis_index("walker")
    c = lax.rem(blk, 2)
    x = lax.rem(lax.div(blk, 2), X)
    y = lax.div(blk, 2 * X)
    yh = lax.rem(wlk, YH)
    z = lax.div(wlk, YH)
    oc = 1 - c
    xp, xm, xo = lax.rem(x + 1, X), lax.rem(x + X - 1, X), lax.rem(x + 2, X)
    y1 = y - 1 + 2 * lax.div(Y - y, Y)
    y3 = (Y - 1) * (1 - lax.div(y, 2))
    ys = [y, y1, 6 - y - y1 - y3, y3]

    def shard(yy, xx, cc):
        return (yy * X + xx) * 2 + cc

    def dev(yy, xx, cc, zz, hh):
        return {"block": shard(yy, xx, cc), "walker": zz * YH + hh}

    def zat(offset):
        return lax.rem(z + offset + Z, Z)

    green_copy = pltpu.make_async_copy(green, gin, local_sem.at[0])
    green_copy.start()
    chol_copy = pltpu.make_async_copy(chol, cbuf, local_sem.at[1])
    chol_copy.start()

    y8 = yh * Y + y

    def ydev(offset):
        at = lax.rem(y8 + offset + YH * Y, YH * Y)
        return dev(lax.rem(at, Y), x, c, z, lax.div(at, Y))

    xc_peers = [dev(y, lax.rem(x + dx, X), cc, z, yh) for dx in (2, 1, 3, 0) for cc in (oc, c)][:7]
    y_peers = [ydev(i) for i in (4, 3, 5, 2, 6, 1, 7)]
    z_peers = [dev(y, x, c, zat(i), yh) for i in (6, 5, 7, 4, 8, 3, 9, 2, 10, 1, 11)]
    xpd, xmd, pd = dev(y, xp, c, z, yh), dev(y, xm, c, z, yh), dev(y, x, oc, z, yh)
    ypd, ymd = ydev(1), ydev(-1)
    zpd, zmd = dev(y, x, c, zat(1), yh), dev(y, x, c, zat(-1), yh)
    near = [xpd, xmd, pd, ypd, ymd, zpd, zmd]
    barrier = pltpu.get_barrier_semaphore()
    for peer in near:
        pl.semaphore_signal(barrier, inc=1, device_id=peer, device_id_type=MESH)

    sent = []

    def send(src, dst, rsem, device, cond=None):
        index = len(sent)

        def make():
            return pltpu.make_async_remote_copy(
                src_ref=src(), dst_ref=dst(), send_sem=send_sem.at[index], recv_sem=rsem(),
                device_id=device, device_id_type=MESH,
            )

        sent.append((make, cond))
        if cond is None:
            make().start()
        else:
            pl.when(cond)(lambda: make().start())

    def both(ref, rsem, device, cond=None):
        send(ref, ref, rsem, device, cond)

    def arrive(dst, rsem, device):
        pltpu.make_async_remote_copy(
            src_ref=dst, dst_ref=dst, send_sem=send_sem.at[0], recv_sem=rsem,
            device_id=device, device_id_type=MESH,
        ).wait_recv()

    green_copy.wait()
    x32[0:SLOTS, :] = gin[...].astype(F32)
    s32[24:32, :] = jnp.zeros((8, NORB), F32)
    for r in range(ROWS):
        s32[SLOTS * r : SLOTS * r + SLOTS, :] = x32[0:SLOTS, NORB * r : NORB * r + NORB]
    gbuf[blk] = s32[...].astype(BF)

    pl.semaphore_wait(barrier, len(near))

    def half(b, h):
        return lambda: gbuf.at[b, 16 * h : 16 * h + 16]

    def whole(b):
        return lambda: gbuf.at[b]

    def sem(b, h):
        return lambda: rg.at[b, h]

    def forward(i, cond=None):
        b = shard(ys[i], x, c)
        if i == 0:
            up, down = y < Y - 1, y > 0
        else:
            up, down = (ys[i] < y) & (y < Y - 1), (ys[i] > y) & (y > 0)
        if cond is not None:
            up, down = up & cond, down & cond
        for h in range(2):
            part = gbuf.at[b, 16 * h : 16 * h + 16]
            if i > 0 and cond is None:
                arrive(part, rg.at[b, h], pd)
            elif i > 0:
                pl.when(cond)(lambda: arrive(part, rg.at[b, h], pd))
            both(half(b, h), sem(b, h), ypd, up)
            both(half(b, h), sem(b, h), ymd, down)
            both(half(b, h), sem(b, h), xpd, cond)
        for h in (1, 0):
            both(half(b, h), sem(b, h), xmd, cond)
        both(whole(b), sem(b, 0), pd, cond)

    def relay(i):
        b = shard(ys[i], xm, c)
        arrive(gbuf.at[b, 0:16], rg.at[b, 0], pd)
        both(half(b, 0), sem(b, 0), xpd)
        b = shard(ys[i], xp, c)
        arrive(gbuf.at[b, 16:32], rg.at[b, 1], pd)
        both(half(b, 1), sem(b, 1), xmd)

    def rest(i):
        b = shard(ys[i], xm, c)
        arrive(gbuf.at[b, 16:32], rg.at[b, 1], pd)
        both(whole(b), sem(b, 0), pd)
        b = shard(ys[i], xp, c)
        arrive(gbuf.at[b, 0:16], rg.at[b, 0], pd)
        both(whole(b), sem(b, 0), pd)
        b = shard(ys[i], xo, c)
        arrive(gbuf.at[b, 0:16], rg.at[b, 0], pd)
        arrive(gbuf.at[b, 16:32], rg.at[b, 1], pd)
        both(whole(b), sem(b, 0), pd)

    def other_core(i):
        for xx in (x, xm, xp, xo):
            b = shard(ys[i], xx, oc)
            arrive(gbuf.at[b], rg.at[b, 0], pd)

    def zsend():
        for device in z_peers:
            both(lambda: lbuf.at[z], lambda: rl.at[z], device)

    def zarrive():
        for i in range(1, Z):
            arrive(lbuf.at[zat(i)], rl.at[zat(i)], pd)

    def hello(i):
        for device in (ypd, ymd, zpd, zmd):
            pl.semaphore_signal(hyz.at[i], inc=1, device_id=device, device_id_type=MESH)

    def heard(i):
        pl.semaphore_wait(hyz.at[i], 4)

    forward(0)
    hello(0)

    for s in range(SLOTS):
        for r in range(LINES):
            g72[s, r : r + 1, :] = x32[s : s + 1, 128 * r : 128 * r + 128]
    for j in range(2):
        lbuf[z, j] = g72[jnp.maximum(mslot[j, wlk], 0)].astype(BF)

    partner = wlk + 1 - 2 * yh
    zero = jnp.int32(0)

    def scan(d, carry):
        own, n, other, m = carry
        for j in range(2):
            dest = mdest[j, d]
            live = mslot[j, d] >= 0
            hit = jnp.where(live & (dest == wlk), 1, 0)
            own = tuple(jnp.where((hit == 1) & (n == a), d * 2 + j, own[a]) for a in range(KEEP))
            n = n + hit
            hit = jnp.where(live & (dest == partner), 1, 0)
            other = tuple(jnp.where((hit == 1) & (m == a), d * 2 + j, other[a]) for a in range(KEEP))
            m = m + hit
        return own, n, other, m

    own, _, other, _ = lax.fori_loop(
        0, Z * YH, scan, ((zero,) * KEEP, zero, (zero,) * KEEP, zero)
    )
    stay_total = zero
    stay = [zero] * KEEP
    for s in range(SLOTS):
        hit = jnp.where((s < counts[wlk]) & (mslot[0, wlk] != s) & (mslot[1, wlk] != s), 1, 0)
        stay = [jnp.where((hit == 1) & (stay_total == t), s, stay[t]) for t in range(KEEP)]
        stay_total = stay_total + hit

    row_id = lax.broadcasted_iota(jnp.int32, (240, 256), 0)
    col_id = lax.broadcasted_iota(jnp.int32, (240, 256), 1)
    inner = jnp.bitwise_and(col_id, 31)
    rr = jnp.right_shift(inner * 13, 6)
    target = (inner - SLOTS * rr) * 48 + jnp.right_shift(col_id, 5) * ROWS + rr
    pick = jnp.where((row_id == target) & (inner < 30), 1.0, 0.0).astype(BF)

    def gather_rows(i):
        a = gbuf[pl.ds(ys[i] * 8, 8)].reshape(256, NORB)
        for kc in range(6):
            cols = slice(256 * kc, 256 * kc + 256)
            gc[:, cols] = jnp.dot(pick, a[:, cols], preferred_element_type=F32).astype(BF)

    def multiply(i, h):
        rows = pl.ds(pl.multiple_of(ys[i] * 48, 16), 48)
        g = 4 * h
        w = jnp.concatenate(
            [
                cbuf[g], cbuf[g + 1, 128:192], cbuf[g + 1, 0:128],
                cbuf[g + 2], cbuf[g + 3, 128:192], cbuf[g + 3, 0:128],
            ],
            0,
        )
        t = lax.dot_general(gc[...], w, NT, preferred_element_type=F32)
        for s in range(SLOTS):
            tbuf[h, s, rows, :] = t[48 * s : 48 * s + 48]

    inside, edge = (y > 0) & (y < Y - 1), (y == 0) | (y == Y - 1)
    heard(0)
    hello(1)
    forward(1)
    forward(2, inside)
    heard(1)
    hello(2)
    relay(0)
    heard(2)
    hello(3)
    rest(0)
    heard(3)
    hello(4)
    forward(2, edge)
    forward(3, inside)
    heard(4)
    relay(1)
    zsend()
    other_core(0)
    chol_copy.wait()
    gather_rows(0)
    rest(1)
    multiply(0, 0)
    forward(3, edge)
    relay(2)
    multiply(0, 1)
    other_core(1)
    gather_rows(1)
    rest(2)
    multiply(1, 0)
    relay(3)
    multiply(1, 1)
    other_core(2)
    gather_rows(2)
    rest(3)
    multiply(2, 0)
    multiply(2, 1)
    zarrive()
    for a in range(KEEP):
        xsend[a] = lbuf[lax.div(other[a], 4), lax.rem(other[a], 2)]
    other_core(3)
    gather_rows(3)
    send(lambda: xsend, lambda: xrecv, lambda: rx.at[0], dev(y, x, c, z, 1 - yh))
    multiply(3, 0)
    multiply(3, 1)

    lane = lax.broadcasted_iota(jnp.int32, (1, 128), 1)
    part = jnp.zeros((1, 128), F32)
    tots = [trace_half(tbuf[0, s]) for s in range(SLOTS)]
    for s in range(SLOTS):
        tot = tots[s] + trace_half(tbuf[1, s])
        value = jnp.sum(jnp.sum(tot, axis=0, keepdims=True), axis=1, keepdims=True)
        part = jnp.where(lane == s, value, part)

    def exchange(buf, sem, me, value, targets, sources):
        buf[me] = value
        for device in targets:
            both(lambda: buf.at[me], lambda: sem.at[me], device)
        for src in sources:
            arrive(buf.at[src], sem.at[src], pd)

    exchange(
        ea, ra, x * 2 + c, part, xc_peers,
        [lax.rem(x + dx, X) * 2 + cc for dx in range(X) for cc in (c, oc)][1:],
    )
    total = ea[0]
    for i in range(1, 2 * X):
        total = total + ea[i]
    exchange(
        eb, rb, y8, total, y_peers,
        [lax.rem(y8 + i, YH * Y) for i in range(1, YH * Y)],
    )
    first = eb[0] + eb[1] + eb[2] + eb[3]
    second = eb[4] + eb[5] + eb[6] + eb[7]
    row = first + pltpu.roll(second, 8, 1)
    ec[z] = row
    for device in z_peers:
        both(lambda: ec.at[z], lambda: rc.at[z], device)

    arrive(xrecv, rx.at[0], pd)
    scale = 0.5 / (NOCC * math.sqrt(256.0))
    found = []
    for t in range(KEEP):
        stays = t < stay_total
        rank = jnp.clip(t - stay_total, 0, KEEP - 1)
        pick_id = own[0]
        for a in range(1, KEEP):
            pick_id = jnp.where(rank == a, own[a], pick_id)
        src_z = lax.div(pick_id, 4)
        src_h = lax.rem(lax.div(pick_id, 2), 2)
        src_j = lax.rem(pick_id, 2)
        moved = jnp.where(src_h == yh, lbuf[src_z, src_j].astype(F32), xrecv[rank].astype(F32))
        line[t] = jnp.where(stays, g72[stay[t]], moved)
        for r in range(LINES):
            n32[t : t + 1, 128 * r : 128 * r + 128] = line[t, r : r + 1, :]
        from_z = jnp.where(stays, z, src_z)
        from_h = jnp.where(stays, yh, src_h)
        from_s = jnp.where(stays, stay[t], jnp.maximum(mslot[src_j, src_z * 2 + src_h], 0))
        found.append((from_z, from_h * 8 + from_s))
    nout[...] = n32[0:KEEP, :].astype(BF)
    new_copy = pltpu.make_async_copy(nout, new_ref, local_sem.at[2])
    new_copy.start()
    for i in range(1, Z):
        arrive(ec.at[zat(i)], rc.at[zat(i)], pd)
    for t, (from_z, at) in enumerate(found):
        en_ref[t] = -scale * jnp.sum(jnp.where(lane == at, ec[from_z], 0.0))
    new_copy.wait()

    for make, cond in sent:
        if cond is None:
            make().wait_send()
        else:
            pl.when(cond)(lambda make=make: make().wait_send())


def finish(new_in, en_in, new_out, en_out):
    new_out[...] = new_in[...]
    for t in range(KEEP):
        en_out[t] = en_in[t]


def body(green, chol, counts, move_slot, move_dest):
    hbm = pl.BlockSpec(memory_space=pl.ANY)
    smem = pl.BlockSpec(memory_space=pltpu.SMEM)
    new, energy = pl.pallas_call(
        kernel,
        out_shape=(
            jax.ShapeDtypeStruct((KEEP, SHARE), BF),
            jax.ShapeDtypeStruct((KEEP,), F32),
        ),
        in_specs=[hbm, hbm, smem, smem, smem],
        out_specs=(hbm, smem),
        scratch_shapes=[
            pltpu.VMEM((SLOTS, SHARE), BF),
            pltpu.VMEM((8, SHARE), F32),
            pltpu.VMEM((32, NORB), F32),
            pltpu.VMEM((SLOTS, LINES, 128), F32),
            pltpu.VMEM((KEEP, LINES, 128), F32),
            pltpu.VMEM((8, SHARE), F32),
            pltpu.VMEM((KEEP, SHARE), BF),
            pltpu.VMEM((32, 32, NORB), BF),
            pltpu.VMEM((Z, 2, LINES, 128), BF),
            pltpu.VMEM((KEEP, LINES, 128), BF),
            pltpu.VMEM((KEEP, LINES, 128), BF),
            pltpu.VMEM((8, NOCC, NORB), BF),
            pltpu.VMEM((240, NORB), BF),
            pltpu.VMEM((2, SLOTS, NOCC, 768), F32),
            pltpu.VMEM((2 * X, 1, 128), F32),
            pltpu.VMEM((YH * Y, 1, 128), F32),
            pltpu.VMEM((Z, 1, 128), F32),
            pltpu.SemaphoreType.DMA((3,)),
            pltpu.SemaphoreType.DMA((140,)),
            pltpu.SemaphoreType.DMA((32, 2)),
            pltpu.SemaphoreType.DMA((Z,)),
            pltpu.SemaphoreType.DMA((2 * X,)),
            pltpu.SemaphoreType.DMA((YH * Y,)),
            pltpu.SemaphoreType.DMA((Z,)),
            pltpu.SemaphoreType.DMA((1,)),
            pltpu.SemaphoreType.REGULAR((5,)),
        ],
        compiler_params=pltpu.CompilerParams(
            collective_id=0, has_side_effects=True, vmem_limit_bytes=60 << 20
        ),
        name="exchange_energy",
    )(green, chol, counts, move_slot.T, move_dest.T)
    vmem = pl.BlockSpec(memory_space=pltpu.VMEM)
    return pl.pallas_call(
        finish,
        out_shape=(
            jax.ShapeDtypeStruct((KEEP, SHARE), BF),
            jax.ShapeDtypeStruct((KEEP,), F32),
        ),
        in_specs=[vmem, smem],
        out_specs=(vmem, smem),
        name="finish",
    )(new, energy)


def solution(mesh):
    in_specs = (P("walker", "block"), P("block", None, None), P(), P(), P())
    out_specs = (P("walker", "block"), P("walker"))
    return jax.shard_map(body, mesh=mesh, in_specs=in_specs, out_specs=out_specs, check_vma=False)
```

```python
import math

import jax
import jax.numpy as jnp
from jax import lax
from jax.experimental import pallas as pl
from jax.experimental.pallas import tpu as pltpu
from jax.sharding import PartitionSpec as P

MESH = pl.DeviceIdType.MESH
NT = (((1,), (1,)), ((), ()))
BF = jnp.bfloat16
F32 = jnp.float32
SLOTS = 5
KEEP = 3
X, Y, YH, Z = 4, 4, 2, 12
ROWS = 6
NORB = 1536
NOCC = 192
SHARE = ROWS * NORB
LINES = SHARE // 128


def trace_half(t):
    acc = jnp.zeros((64, 128), F32)
    corners = []
    for pair in range(2):
        t0 = t[:, 384 * pair : 384 * pair + 128]
        t1 = t[:, 384 * pair + 128 : 384 * pair + 256]
        t2 = t[:, 384 * pair + 256 : 384 * pair + 384]
        for a in (t0[0:128], t2[0:128]):
            m = a * a.T
            acc = acc + m[0:64] + m[64:128]
        b = t1[0:128].T
        acc = acc + 2.0 * (b[0:64] * t0[128:192] + b[64:128] * t2[128:192])
        corners.append(t1[128:192])
    e = jnp.concatenate(corners, 0)
    et = e.T
    low = lax.broadcasted_iota(jnp.int32, (64, 128), 1) < 64
    r0 = pltpu.roll(et[0:64], 64, 1)
    r1 = pltpu.roll(et[64:128], 64, 1)
    acc = acc + e[0:64] * jnp.where(low, et[0:64], r1)
    return acc + e[64:128] * jnp.where(low, r0, et[64:128])


def kernel(
    green, chol, counts, mslot, mdest, new_ref, en_ref,
    gin, x32, s32, g72, line, n32, nout, gbuf, lbuf, xsend, xrecv, cbuf, gc, tbuf, ea, eb, ec,
    local_sem, send_sem, rg, rl, ra, rb, rc, rx, hyz,
):
    blk = lax.axis_index("block")
    wlk = lax.axis_index("walker")
    c = lax.rem(blk, 2)
    x = lax.rem(lax.div(blk, 2), X)
    y = lax.div(blk, 2 * X)
    yh = lax.rem(wlk, YH)
    z = lax.div(wlk, YH)
    oc = 1 - c
    xp, xm, xo = lax.rem(x + 1, X), lax.rem(x + X - 1, X), lax.rem(x + 2, X)
    y1 = y - 1 + 2 * lax.div(Y - y, Y)
    y3 = (Y - 1) * (1 - lax.div(y, 2))
    ys = [y, y1, 6 - y - y1 - y3, y3]

    def shard(yy, xx, cc):
        return (yy * X + xx) * 2 + cc

    def dev(yy, xx, cc, zz, hh):
        return {"block": shard(yy, xx, cc), "walker": zz * YH + hh}

    def zat(offset):
        return lax.rem(z + offset + Z, Z)

    green_copy = pltpu.make_async_copy(green, gin, local_sem.at[0])
    green_copy.start()
    chol_copy = pltpu.make_async_copy(chol, cbuf, local_sem.at[1])
    chol_copy.start()

    y8 = yh * Y + y

    def ydev(offset):
        at = lax.rem(y8 + offset + YH * Y, YH * Y)
        return dev(lax.rem(at, Y), x, c, z, lax.div(at, Y))

    xc_peers = [dev(y, lax.rem(x + dx, X), cc, z, yh) for dx in (2, 1, 3, 0) for cc in (oc, c)][:7]
    y_peers = [ydev(i) for i in (4, 3, 5, 2, 6, 1, 7)]
    z_peers = [dev(y, x, c, zat(i), yh) for i in (6, 5, 7, 4, 8, 3, 9, 2, 10, 1, 11)]
    xpd, xmd, pd = dev(y, xp, c, z, yh), dev(y, xm, c, z, yh), dev(y, x, oc, z, yh)
    ypd, ymd = ydev(1), ydev(-1)
    zpd, zmd = dev(y, x, c, zat(1), yh), dev(y, x, c, zat(-1), yh)
    near = [xpd, xmd, pd, ypd, ymd, zpd, zmd]
    barrier = pltpu.get_barrier_semaphore()
    for peer in near:
        pl.semaphore_signal(barrier, inc=1, device_id=peer, device_id_type=MESH)

    sent = []

    def send(src, dst, rsem, device, cond=None):
        index = len(sent)

        def make():
            return pltpu.make_async_remote_copy(
                src_ref=src(), dst_ref=dst(), send_sem=send_sem.at[index], recv_sem=rsem(),
                device_id=device, device_id_type=MESH,
            )

        sent.append((make, cond))
        if cond is None:
            make().start()
        else:
            pl.when(cond)(lambda: make().start())

    def both(ref, rsem, device, cond=None):
        send(ref, ref, rsem, device, cond)

    def arrive(dst, rsem, device):
        pltpu.make_async_remote_copy(
            src_ref=dst, dst_ref=dst, send_sem=send_sem.at[0], recv_sem=rsem,
            device_id=device, device_id_type=MESH,
        ).wait_recv()

    green_copy.wait()
    x32[0:SLOTS, :] = gin[...].astype(F32)
    s32[24:32, :] = jnp.zeros((8, NORB), F32)
    for r in range(ROWS):
        s32[SLOTS * r : SLOTS * r + SLOTS, :] = x32[0:SLOTS, NORB * r : NORB * r + NORB]
    gbuf[blk] = s32[...].astype(BF)

    pl.semaphore_wait(barrier, len(near))

    def half(b, h):
        return lambda: gbuf.at[b, 16 * h : 16 * h + 16]

    def whole(b):
        return lambda: gbuf.at[b]

    def sem(b, h):
        return lambda: rg.at[b, h]

    def forward(i, cond=None):
        b = shard(ys[i], x, c)
        if i == 0:
            up, down = y < Y - 1, y > 0
        else:
            up, down = (ys[i] < y) & (y < Y - 1), (ys[i] > y) & (y > 0)
        if cond is not None:
            up, down = up & cond, down & cond
        for h in range(2):
            part = gbuf.at[b, 16 * h : 16 * h + 16]
            if i > 0 and cond is None:
                arrive(part, rg.at[b, h], pd)
            elif i > 0:
                pl.when(cond)(lambda: arrive(part, rg.at[b, h], pd))
            both(half(b, h), sem(b, h), ypd, up)
            both(half(b, h), sem(b, h), ymd, down)
            both(half(b, h), sem(b, h), xpd, cond)
        for h in (1, 0):
            both(half(b, h), sem(b, h), xmd, cond)
        both(whole(b), sem(b, 0), pd, cond)

    def relay(i):
        b = shard(ys[i], xm, c)
        arrive(gbuf.at[b, 0:16], rg.at[b, 0], pd)
        both(half(b, 0), sem(b, 0), xpd)
        b = shard(ys[i], xp, c)
        arrive(gbuf.at[b, 16:32], rg.at[b, 1], pd)
        both(half(b, 1), sem(b, 1), xmd)

    def rest(i):
        b = shard(ys[i], xm, c)
        arrive(gbuf.at[b, 16:32], rg.at[b, 1], pd)
        both(whole(b), sem(b, 0), pd)
        b = shard(ys[i], xp, c)
        arrive(gbuf.at[b, 0:16], rg.at[b, 0], pd)
        both(whole(b), sem(b, 0), pd)
        b = shard(ys[i], xo, c)
        arrive(gbuf.at[b, 0:16], rg.at[b, 0], pd)
        arrive(gbuf.at[b, 16:32], rg.at[b, 1], pd)
        both(whole(b), sem(b, 0), pd)

    def other_core(i):
        for xx in (x, xm, xp, xo):
            b = shard(ys[i], xx, oc)
            arrive(gbuf.at[b], rg.at[b, 0], pd)

    def zsend():
        for device in z_peers:
            both(lambda: lbuf.at[z], lambda: rl.at[z], device)

    def zarrive():
        for i in range(1, Z):
            arrive(lbuf.at[zat(i)], rl.at[zat(i)], pd)

    def hello(i):
        for device in (ypd, ymd, zpd, zmd):
            pl.semaphore_signal(hyz.at[i], inc=1, device_id=device, device_id_type=MESH)

    def heard(i):
        pl.semaphore_wait(hyz.at[i], 4)

    forward(0)
    hello(0)

    for s in range(SLOTS):
        for r in range(LINES):
            g72[s, r : r + 1, :] = x32[s : s + 1, 128 * r : 128 * r + 128]
    for j in range(2):
        lbuf[z, j] = g72[jnp.maximum(mslot[j, wlk], 0)].astype(BF)

    partner = wlk + 1 - 2 * yh
    zero = jnp.int32(0)

    def scan(d, carry):
        own, n, other, m = carry
        for j in range(2):
            dest = mdest[j, d]
            live = mslot[j, d] >= 0
            hit = jnp.where(live & (dest == wlk), 1, 0)
            own = tuple(jnp.where((hit == 1) & (n == a), d * 2 + j, own[a]) for a in range(KEEP))
            n = n + hit
            hit = jnp.where(live & (dest == partner), 1, 0)
            other = tuple(jnp.where((hit == 1) & (m == a), d * 2 + j, other[a]) for a in range(KEEP))
            m = m + hit
        return own, n, other, m

    own, _, other, _ = lax.fori_loop(
        0, Z * YH, scan, ((zero,) * KEEP, zero, (zero,) * KEEP, zero)
    )
    stay_total = zero
    stay = [zero] * KEEP
    for s in range(SLOTS):
        hit = jnp.where((s < counts[wlk]) & (mslot[0, wlk] != s) & (mslot[1, wlk] != s), 1, 0)
        stay = [jnp.where((hit == 1) & (stay_total == t), s, stay[t]) for t in range(KEEP)]
        stay_total = stay_total + hit

    row_id = lax.broadcasted_iota(jnp.int32, (240, 256), 0)
    col_id = lax.broadcasted_iota(jnp.int32, (240, 256), 1)
    inner = jnp.bitwise_and(col_id, 31)
    rr = jnp.right_shift(inner * 13, 6)
    target = (inner - SLOTS * rr) * 48 + jnp.right_shift(col_id, 5) * ROWS + rr
    pick = jnp.where((row_id == target) & (inner < 30), 1.0, 0.0).astype(BF)

    def gather_rows(i):
        a = gbuf[pl.ds(ys[i] * 8, 8)].reshape(256, NORB)
        for kc in range(6):
            cols = slice(256 * kc, 256 * kc + 256)
            gc[:, cols] = jnp.dot(pick, a[:, cols], preferred_element_type=F32).astype(BF)

    def multiply(i, h):
        rows = pl.ds(pl.multiple_of(ys[i] * 48, 16), 48)
        g = 4 * h
        w = jnp.concatenate(
            [
                cbuf[g], cbuf[g + 1, 128:192], cbuf[g + 1, 0:128],
                cbuf[g + 2], cbuf[g + 3, 128:192], cbuf[g + 3, 0:128],
            ],
            0,
        )
        t = lax.dot_general(gc[...], w, NT, preferred_element_type=F32)
        for s in range(SLOTS):
            tbuf[h, s, rows, :] = t[48 * s : 48 * s + 48]

    inside, edge = (y > 0) & (y < Y - 1), (y == 0) | (y == Y - 1)
    heard(0)
    hello(1)
    forward(1)
    forward(2, inside)
    heard(1)
    hello(2)
    relay(0)
    heard(2)
    hello(3)
    rest(0)
    heard(3)
    hello(4)
    forward(2, edge)
    forward(3, inside)
    heard(4)
    relay(1)
    zsend()
    other_core(0)
    chol_copy.wait()
    gather_rows(0)
    rest(1)
    multiply(0, 0)
    forward(3, edge)
    relay(2)
    multiply(0, 1)
    other_core(1)
    gather_rows(1)
    rest(2)
    multiply(1, 0)
    relay(3)
    multiply(1, 1)
    other_core(2)
    gather_rows(2)
    rest(3)
    multiply(2, 0)
    multiply(2, 1)
    other_core(3)
    gather_rows(3)
    multiply(3, 0)
    multiply(3, 1)

    lane = lax.broadcasted_iota(jnp.int32, (1, 128), 1)
    part = jnp.zeros((1, 128), F32)
    tots = [trace_half(tbuf[0, s]) for s in range(SLOTS)]
    for s in range(SLOTS):
        tot = tots[s] + trace_half(tbuf[1, s])
        value = jnp.sum(jnp.sum(tot, axis=0, keepdims=True), axis=1, keepdims=True)
        part = jnp.where(lane == s, value, part)

    def exchange(buf, sem, me, value, targets, sources, between=None):
        buf[me] = value
        for device in targets:
            both(lambda: buf.at[me], lambda: sem.at[me], device)
        if between is not None:
            between()
        for src in sources:
            arrive(buf.at[src], sem.at[src], pd)

    def partner_rows():
        zarrive()
        for a in range(KEEP):
            xsend[a] = lbuf[lax.div(other[a], 4), lax.rem(other[a], 2)]
        send(lambda: xsend, lambda: xrecv, lambda: rx.at[0], dev(y, x, c, z, 1 - yh))

    exchange(
        ea, ra, x * 2 + c, part, xc_peers,
        [lax.rem(x + dx, X) * 2 + cc for dx in range(X) for cc in (c, oc)][1:],
        partner_rows,
    )
    total = ea[0]
    for i in range(1, 2 * X):
        total = total + ea[i]
    exchange(
        eb, rb, y8, total, y_peers,
        [lax.rem(y8 + i, YH * Y) for i in range(1, YH * Y)],
    )
    first = eb[0] + eb[1] + eb[2] + eb[3]
    second = eb[4] + eb[5] + eb[6] + eb[7]
    row = first + pltpu.roll(second, 8, 1)
    ec[z] = row
    for device in z_peers:
        both(lambda: ec.at[z], lambda: rc.at[z], device)

    arrive(xrecv, rx.at[0], pd)
    scale = 0.5 / (NOCC * math.sqrt(256.0))
    found = []
    for t in range(KEEP):
        stays = t < stay_total
        rank = jnp.clip(t - stay_total, 0, KEEP - 1)
        pick_id = own[0]
        for a in range(1, KEEP):
            pick_id = jnp.where(rank == a, own[a], pick_id)
        src_z = lax.div(pick_id, 4)
        src_h = lax.rem(lax.div(pick_id, 2), 2)
        src_j = lax.rem(pick_id, 2)
        moved = jnp.where(src_h == yh, lbuf[src_z, src_j].astype(F32), xrecv[rank].astype(F32))
        line[t] = jnp.where(stays, g72[stay[t]], moved)
        for r in range(LINES):
            n32[t : t + 1, 128 * r : 128 * r + 128] = line[t, r : r + 1, :]
        from_z = jnp.where(stays, z, src_z)
        from_h = jnp.where(stays, yh, src_h)
        from_s = jnp.where(stays, stay[t], jnp.maximum(mslot[src_j, src_z * 2 + src_h], 0))
        found.append((from_z, from_h * 8 + from_s))
    nout[...] = n32[0:KEEP, :].astype(BF)
    new_copy = pltpu.make_async_copy(nout, new_ref, local_sem.at[2])
    new_copy.start()
    for i in range(1, Z):
        arrive(ec.at[zat(i)], rc.at[zat(i)], pd)
    for t, (from_z, at) in enumerate(found):
        en_ref[t] = -scale * jnp.sum(jnp.where(lane == at, ec[from_z], 0.0))
    new_copy.wait()

    for make, cond in sent:
        if cond is None:
            make().wait_send()
        else:
            pl.when(cond)(lambda make=make: make().wait_send())


def finish(new_in, en_in, new_out, en_out):
    new_out[...] = new_in[...]
    for t in range(KEEP):
        en_out[t] = en_in[t]


def body(green, chol, counts, move_slot, move_dest):
    hbm = pl.BlockSpec(memory_space=pl.ANY)
    smem = pl.BlockSpec(memory_space=pltpu.SMEM)
    new, energy = pl.pallas_call(
        kernel,
        out_shape=(
            jax.ShapeDtypeStruct((KEEP, SHARE), BF),
            jax.ShapeDtypeStruct((KEEP,), F32),
        ),
        in_specs=[hbm, hbm, smem, smem, smem],
        out_specs=(hbm, smem),
        scratch_shapes=[
            pltpu.VMEM((SLOTS, SHARE), BF),
            pltpu.VMEM((8, SHARE), F32),
            pltpu.VMEM((32, NORB), F32),
            pltpu.VMEM((SLOTS, LINES, 128), F32),
            pltpu.VMEM((KEEP, LINES, 128), F32),
            pltpu.VMEM((8, SHARE), F32),
            pltpu.VMEM((KEEP, SHARE), BF),
            pltpu.VMEM((32, 32, NORB), BF),
            pltpu.VMEM((Z, 2, LINES, 128), BF),
            pltpu.VMEM((KEEP, LINES, 128), BF),
            pltpu.VMEM((KEEP, LINES, 128), BF),
            pltpu.VMEM((8, NOCC, NORB), BF),
            pltpu.VMEM((240, NORB), BF),
            pltpu.VMEM((2, SLOTS, NOCC, 768), F32),
            pltpu.VMEM((2 * X, 1, 128), F32),
            pltpu.VMEM((YH * Y, 1, 128), F32),
            pltpu.VMEM((Z, 1, 128), F32),
            pltpu.SemaphoreType.DMA((3,)),
            pltpu.SemaphoreType.DMA((140,)),
            pltpu.SemaphoreType.DMA((32, 2)),
            pltpu.SemaphoreType.DMA((Z,)),
            pltpu.SemaphoreType.DMA((2 * X,)),
            pltpu.SemaphoreType.DMA((YH * Y,)),
            pltpu.SemaphoreType.DMA((Z,)),
            pltpu.SemaphoreType.DMA((1,)),
            pltpu.SemaphoreType.REGULAR((5,)),
        ],
        compiler_params=pltpu.CompilerParams(
            collective_id=0, has_side_effects=True, vmem_limit_bytes=60 << 20
        ),
        name="exchange_energy",
    )(green, chol, counts, move_slot.T, move_dest.T)
    vmem = pl.BlockSpec(memory_space=pltpu.VMEM)
    return pl.pallas_call(
        finish,
        out_shape=(
            jax.ShapeDtypeStruct((KEEP, SHARE), BF),
            jax.ShapeDtypeStruct((KEEP,), F32),
        ),
        in_specs=[vmem, smem],
        out_specs=(vmem, smem),
        name="finish",
    )(new, energy)


def solution(mesh):
    in_specs = (P("walker", "block"), P("block", None, None), P(), P(), P())
    out_specs = (P("walker", "block"), P("walker"))
    return jax.shard_map(body, mesh=mesh, in_specs=in_specs, out_specs=out_specs, check_vma=False)
```
